1024 devices in a mesh: dp: 256 (over y, x_lo, z, core), tensor: 4 (over x_hi).
Axes of the slice: x: 8 (x_hi: 4, x_lo: 2; x = x_hi * 2 + x_lo), y: 8, z: 8, core: 2. Of those that a mesh axis runs over, the one named last changes fastest.
Arguments:
- train_hidden: bfloat16 [256, 128, 28672], P('dp', None, 'tensor'), may hold values from -6 to 6
- train_grad: bfloat16 [256, 128, 8192], P('dp', None, 'tensor'), may hold values from -6 to 6
- test_hidden: bfloat16 [256, 64, 28672], P('dp', None, 'tensor'), may hold values from -6 to 6
- test_grad: bfloat16 [256, 64, 8192], P('dp', None, 'tensor'), may hold values from -6 to 6
- proj_in: bfloat16 [64, 28672], P(None, 'tensor'), may hold values from -0.03125 to 0.03125
- proj_out: bfloat16 [64, 8192], P(None, 'tensor'), may hold values from -0.0625 to 0.0625
- precond_in: float32 [64, 64], replicated, may hold values from -0.75 to 0.75
- precond_out: float32 [64, 64], replicated, may hold values from -0.75 to 0.75
Outputs:
- scores: float32 [256, 256], P('dp', 'tensor')
The draws below stay inside these ranges and needn't reach their ends.
All inputs are finite; a program needn't handle non-finite values.
Results may differ from the reference program's by a relative error of at most 0.0029.
Values may be sent and summed in bfloat16 or wider, within the bound.
No kernel may reach another device: no remote copies, remote signals or barrier semaphores. Data moves between devices by JAX's collectives and lax.ppermute only.
A program may use at most 32 MiB of HBM per device.

```python
import math
import jax
import jax.numpy as jnp
from jax import lax

D = 8192
FF = 28672
RANK = 64
SEQ = 128
QRY_TOK = 64
EXAMPLES = 256
QUERIES = 256


def steps_of(rng, extent, pieces, low, top_value):
    level, own = 1.0, jax.random.fold_in(rng, 6)
    for dim, shards_of in pieces:
        heights = jnp.exp(jax.random.uniform(jax.random.fold_in(own, dim), (shards_of,), jnp.float32, low / len(pieces), top_value / len(pieces)))
        level = level * jnp.repeat(heights, extent[dim] // shards_of).reshape([-1 if axis == dim else 1 for axis in range(len(extent))])
    return level


def centred(own_key, dims, deviation, bound, pieces=(), dtype=jnp.bfloat16):
    gain = steps_of(own_key, dims, pieces, -0.22, 0.18) if pieces else 1.0
    entries = jax.random.normal(own_key, dims, jnp.float32) * deviation * gain
    return jnp.minimum(jnp.maximum(entries, -bound), bound).astype(dtype)


def setup_inputs(seed: int = 0) -> dict:
    key_list = jax.random.split(jax.random.key(seed), 9)
    return {
        "train_hidden": centred(key_list[0], (EXAMPLES, SEQ, FF), 1.0, 6.0, ((0, 256), (2, 4))),
        "train_grad": centred(key_list[1], (EXAMPLES, SEQ, D), 1.0, 6.0, ((0, 256), (2, 4))),
        "test_hidden": centred(key_list[2], (QUERIES, QRY_TOK, FF), 1.0, 6.0, ((0, 256), (2, 4))),
        "test_grad": centred(key_list[3], (QUERIES, QRY_TOK, D), 1.0, 6.0, ((0, 256), (2, 4))),
        "proj_in": centred(key_list[4], (RANK, FF), FF ** -0.5, 0.03125, ((1, 4),)),
        "proj_out": centred(key_list[5], (RANK, D), D ** -0.5, 0.0625, ((1, 4),)),
        "precond_in": centred(key_list[6], (RANK, RANK), RANK ** -0.5, 0.75, (), jnp.float32),
        "precond_out": centred(key_list[7], (RANK, RANK), RANK ** -0.5, 0.75, (), jnp.float32),
    }


def make_sketch(hidden, grad, proj_in, proj_out):
    left = jnp.dot(hidden, proj_in.T, preferred_element_type=jnp.float32)
    right = jnp.dot(grad, proj_out.T, preferred_element_type=jnp.float32)
    return jnp.dot(left.T, right, precision=lax.Precision.HIGHEST, preferred_element_type=jnp.float32)

def reference(train_hidden, train_grad, test_hidden, test_grad, proj_in, proj_out, precond_in, precond_out):

    def train_one(pair):
        return make_sketch(pair[0], pair[1], proj_in, proj_out)
    train_sketch = lax.map(train_one, (train_hidden, train_grad))
    test_sketch = lax.map(train_one, (test_hidden, test_grad))
    halfway = jnp.einsum('ai,qij->qaj', precond_in, test_sketch, precision=lax.Precision.HIGHEST)
    conditioned = jnp.einsum('qaj,jb->qab', halfway, precond_out, precision=lax.Precision.HIGHEST)
    conditioned = conditioned.astype(jnp.bfloat16)
    factor = 1.0 / (RANK * math.sqrt(SEQ * QRY_TOK))
    scores = jnp.einsum('eab,qab->eq', train_sketch, conditioned.astype(jnp.float32), precision=lax.Precision.HIGHEST)
    return scores * factor
```

```python
import functools
import math

import jax
import jax.numpy as jnp
from jax import lax
from jax.experimental import pallas as pl
from jax.experimental.pallas import tpu as pltpu
from jax.sharding import Mesh, PartitionSpec as P

Y, XL, Z, C, T = 8, 2, 8, 2, 4
OWN = XL * C
LINE = OWN * T
PLANE = Y * Z
F32, BF16 = jnp.float32, jnp.bfloat16
CHUNKS = 4


def nt(a, b, precision=None):
    return lax.dot_general(
        a, b, (((1,), (1,)), ((), ())), precision=precision, preferred_element_type=F32
    )


exact_nt = functools.partial(nt, precision=lax.Precision.HIGHEST)


def lanes_of(shape):
    return lax.broadcasted_iota(jnp.int32, shape, len(shape) - 1)


def rows_of(shape):
    return lax.broadcasted_iota(jnp.int32, shape, 0)


def hi_lo(x):
    hi = x.astype(BF16)
    lo = (x - hi.astype(F32)).astype(BF16)
    return jnp.concatenate([hi, lo], axis=1)


def project_kernel(
    th, tg, qh, qg, pin, pout, cin, cout, send, th_v, tg_v, qh_v, qg_v, pin_v, pout_v, cin_v, cout_v, sems
):
    count = 0
    groups = []

    def fetch(pairs):
        nonlocal count
        started = []
        for src, dst in pairs:
            copy = pltpu.make_async_copy(src, dst, sems.at[count])
            copy.start()
            started.append(copy)
            count += 1
        groups.append(started)

    fetch([(pout, pout_v), (tg.at[0], tg_v), (qg.at[0], qg_v)])
    step = th_v.shape[1] // CHUNKS
    for k in range(CHUNKS):
        cut = pl.ds(k * step, step)
        fetch(
            [
                (pin.at[:, cut], pin_v.at[:, cut]),
                (th.at[0, :, cut], th_v.at[:, cut]),
                (qh.at[0, :, cut], qh_v.at[:, cut]),
            ]
        )
        if k == 0:
            fetch([(cin, cin_v), (cout, cout_v)])

    def wait(group):
        for copy in group:
            copy.wait()

    wait(groups[0])
    right_train = nt(pout_v[...], tg_v[...])
    right_test = nt(pout_v[...], qg_v[...])
    wait(groups[1])
    wait(groups[2])
    right_test = lax.dot_general(
        cout_v[...], right_test, (((0,), (0,)), ((), ())),
        precision=lax.Precision.HIGHEST, preferred_element_type=F32,
    )
    left_train = left_test = None
    for k in range(CHUNKS):
        if k:
            wait(groups[k + 2])
        cut = pl.ds(k * step, step)
        more_train = nt(pin_v[:, cut], th_v[:, cut])
        more_test = nt(pin_v[:, cut], qh_v[:, cut])
        left_train = more_train if k == 0 else left_train + more_train
        left_test = more_test if k == 0 else left_test + more_test
    left_test = jnp.dot(
        cin_v[...], left_test, precision=lax.Precision.HIGHEST, preferred_element_type=F32
    )
    left_train, right_train = left_train.astype(BF16), right_train.astype(BF16)
    left_test, right_test = hi_lo(left_test), hi_lo(right_test)
    for i in range(OWN):
        for j in range(T):
            peer = i * T + j
            send[peer, 0:16] = left_train[16 * i : 16 * i + 16]
            send[peer, 16:32] = right_train[16 * j : 16 * j + 16]
            send[peer, 32:48] = left_test[16 * i : 16 * i + 16]
            send[peer, 48:64] = right_test[16 * j : 16 * j + 16]


def project(th, tg, qh, qg, pin, pout, cin, cout):
    any_space = pl.BlockSpec(memory_space=pl.ANY)
    vmem = lambda a: pltpu.VMEM(a.shape[-2:], a.dtype)
    args = (th, tg, qh, qg, pin, pout, cin, cout)
    return pl.pallas_call(
        project_kernel,
        out_shape=jax.ShapeDtypeStruct((LINE, 64, 128), BF16),
        in_specs=[any_space] * 8,
        out_specs=pl.BlockSpec(memory_space=pltpu.VMEM),
        scratch_shapes=[vmem(a) for a in args] + [pltpu.SemaphoreType.DMA((3 * CHUNKS + 5,))],
        name="project",
    )(*args)


def sketch_kernel(factor, recv, msg, train):
    lane = lanes_of((8, 128))
    lefts, rights = [], []
    for e in range(OWN):
        part = recv[T * e].astype(F32)
        for t in range(1, T):
            part = part + recv[T * e + t].astype(F32)
        left, right = part[0:16], part[16:32]
        block = exact_nt(left, jnp.concatenate([right] * 8, axis=0))
        train[e] = jnp.where(lane < 64, block[0:8], block[8:16]) * factor
        lefts.append(part[32:48])
        rights.append(part[48:64])
    left = jnp.concatenate(lefts, axis=0)
    right = jnp.concatenate(rights, axis=0)
    left = left + pltpu.roll(left, 64, 1)
    right = right + pltpu.roll(right, 64, 1)
    left = jnp.where(lanes_of((64, 128)) < 64, left, 0.0)
    block = exact_nt(left, jnp.concatenate([right, right], axis=0))
    same = rows_of((64, 128)) // 16 == (lanes_of((64, 128)) % 64) // 16
    block = jnp.where(same, block, 0.0)
    block = (block[0:16] + block[16:32]) + (block[32:48] + block[48:64])
    block = jnp.where(lane < 64, block[0:8], block[8:16]).astype(BF16)
    msg[...] = jnp.broadcast_to(block[None], msg.shape)


def sketch(recv, factor):
    vmem = pl.BlockSpec(memory_space=pltpu.VMEM)
    return pl.pallas_call(
        functools.partial(sketch_kernel, factor),
        out_shape=(
            jax.ShapeDtypeStruct((PLANE, 8, 128), BF16),
            jax.ShapeDtypeStruct((OWN, 8, 128), F32),
        ),
        in_specs=[vmem],
        out_specs=(vmem, vmem),
        name="sketch",
    )(recv)


def score_kernel(gathered, train, out, wide):
    wide[...] = gathered[...].astype(F32).reshape(PLANE * 8, 128)
    totals = [None] * OWN
    for r in range(8):
        rows = wide[pl.ds(r, PLANE, stride=8), :]
        for e in range(OWN):
            more = rows * train[e, r : r + 1, :]
            totals[e] = more if r == 0 else totals[e] + more
    total = jnp.concatenate(totals, axis=0)
    row, lane = rows_of((128, 64)), lanes_of((128, 64))
    pick = (row // 16) % OWN == (lane // 16) % XL * C + lane % C
    spread = jnp.dot(
        total, pick.astype(F32), precision=lax.Precision.HIGHEST, preferred_element_type=F32
    )
    row, lane = rows_of((OWN * PLANE, 64)), lanes_of((OWN * PLANE, 64))
    spread = jnp.where(row % 16 == lane // 32 * Z + (lane // C) % Z, spread, 0.0)
    out[...] = jnp.sum(spread.reshape(LINE, 16, 64), axis=1, keepdims=True)


def score(gathered, train):
    vmem = pl.BlockSpec(memory_space=pltpu.VMEM)
    return pl.pallas_call(
        score_kernel,
        out_shape=jax.ShapeDtypeStruct((LINE, 1, 64), F32),
        in_specs=[vmem, vmem],
        out_specs=vmem,
        scratch_shapes=[pltpu.VMEM((PLANE * 8, 128), F32)],
        name="score",
    )(gathered, train)


def exchange(x, axes):
    return lax.all_to_all(x, axes, split_axis=0, concat_axis=0, tiled=True)


def shards(
    train_hidden, train_grad, test_hidden, test_grad, proj_in, proj_out, precond_in, precond_out
):
    rank = proj_in.shape[0]
    factor = 1.0 / (rank * math.sqrt(train_hidden.shape[1] * test_hidden.shape[1]))
    send = project(
        train_hidden, train_grad, test_hidden, test_grad, proj_in, proj_out, precond_in, precond_out
    )
    recv = exchange(send, ("xl", "c", "t"))
    msg, train = sketch(recv, factor)
    gathered = exchange(msg, ("y", "z"))
    partial = score(gathered, train)
    total = exchange(partial, ("xl", "c", "t"))
    return jnp.sum(total, axis=0)


def solution(mesh):
    fine = Mesh(mesh.devices.reshape(Y, XL, Z, C, T), ("y", "xl", "z", "c", "t"))
    dp = ("y", "xl", "z", "c")
    placed = (
        P(dp, None, "t"),
        P(dp, None, "t"),
        P(dp, None, "t"),
        P(dp, None, "t"),
        P(None, "t"),
        P(None, "t"),
        P(),
        P(),
    )
    return jax.shard_map(
        shards, mesh=fine, in_specs=placed, out_specs=P(dp, "t"), check_vma=False
    )
```

```python
import functools
import math

import jax
import jax.numpy as jnp
from jax import lax
from jax.experimental import pallas as pl
from jax.experimental.pallas import tpu as pltpu
from jax.sharding import Mesh, PartitionSpec as P

Y, XL, Z, C, T = 8, 2, 8, 2, 4
OWN = XL * C
LINE = OWN * T
PLANE = Y * Z
F32, BF16 = jnp.float32, jnp.bfloat16
CHUNKS = 4


def nt(a, b, precision=None):
    return lax.dot_general(
        a, b, (((1,), (1,)), ((), ())), precision=precision, preferred_element_type=F32
    )


exact_nt = functools.partial(nt, precision=lax.Precision.HIGHEST)


def lanes_of(shape):
    return lax.broadcasted_iota(jnp.int32, shape, len(shape) - 1)


def rows_of(shape):
    return lax.broadcasted_iota(jnp.int32, shape, 0)


def hi_lo(x):
    hi = x.astype(BF16)
    lo = (x - hi.astype(F32)).astype(BF16)
    return jnp.concatenate([hi, lo], axis=1)


def project_kernel(
    th, tg, qh, qg, pin, pout, cin, cout, send, th_v, tg_v, qh_v, qg_v, pin_v, pout_v, cin_v, cout_v, sems
):
    count = 0
    groups = []

    def fetch(pairs):
        nonlocal count
        started = []
        for src, dst in pairs:
            copy = pltpu.make_async_copy(src, dst, sems.at[count])
            copy.start()
            started.append(copy)
            count += 1
        groups.append(started)

    fetch([(pout, pout_v), (tg.at[0], tg_v), (qg.at[0], qg_v)])
    step = th_v.shape[1] // CHUNKS
    for k in range(CHUNKS):
        cut = pl.ds(k * step, step)
        fetch(
            [
                (pin.at[:, cut], pin_v.at[:, cut]),
                (th.at[0, :, cut], th_v.at[:, cut]),
                (qh.at[0, :, cut], qh_v.at[:, cut]),
            ]
        )
        if k == 0:
            fetch([(cin, cin_v), (cout, cout_v)])

    def wait(group):
        for copy in group:
            copy.wait()

    wait(groups[0])
    right_train = nt(pout_v[...], tg_v[...])
    right_test = nt(pout_v[...], qg_v[...])
    wait(groups[1])
    wait(groups[2])
    right_test = lax.dot_general(
        cout_v[...], right_test, (((0,), (0,)), ((), ())),
        precision=lax.Precision.HIGHEST, preferred_element_type=F32,
    )
    left_train = left_test = None
    for k in range(CHUNKS):
        if k:
            wait(groups[k + 2])
        cut = pl.ds(k * step, step)
        more_train = nt(pin_v[:, cut], th_v[:, cut])
        more_test = nt(pin_v[:, cut], qh_v[:, cut])
        left_train = more_train if k == 0 else left_train + more_train
        left_test = more_test if k == 0 else left_test + more_test
    left_test = jnp.dot(
        cin_v[...], left_test, precision=lax.Precision.HIGHEST, preferred_element_type=F32
    )
    left_train, right_train = left_train.astype(BF16), right_train.astype(BF16)
    left_test, right_test = hi_lo(left_test), hi_lo(right_test)
    for i in range(OWN):
        for j in range(T):
            peer = i * T + j
            send[peer, 0:16] = left_train[16 * i : 16 * i + 16]
            send[peer, 16:32] = right_train[16 * j : 16 * j + 16]
            send[peer, 32:48] = left_test[16 * i : 16 * i + 16]
            send[peer, 48:64] = right_test[16 * j : 16 * j + 16]


def project(th, tg, qh, qg, pin, pout, cin, cout):
    hbm = pl.BlockSpec(memory_space=pltpu.HBM)
    vmem = lambda a: pltpu.VMEM(a.shape[-2:], a.dtype)
    args = [
        pltpu.with_memory_space_constraint(a, pltpu.HBM) for a in (th, tg, qh, qg, pin, pout, cin, cout)
    ]
    return pl.pallas_call(
        project_kernel,
        out_shape=jax.ShapeDtypeStruct((LINE, 64, 128), BF16),
        in_specs=[hbm] * 8,
        out_specs=pl.BlockSpec(memory_space=pltpu.VMEM),
        scratch_shapes=[vmem(a) for a in args] + [pltpu.SemaphoreType.DMA((3 * CHUNKS + 5,))],
        compiler_params=pltpu.CompilerParams(vmem_limit_bytes=12 << 20),
        name="project",
    )(*args)


def sketch_kernel(factor, recv, msg, train):
    lane = lanes_of((8, 128))
    lefts, rights = [], []
    for e in range(OWN):
        part = recv[T * e].astype(F32)
        for t in range(1, T):
            part = part + recv[T * e + t].astype(F32)
        left, right = part[0:16], part[16:32]
        block = exact_nt(left, jnp.concatenate([right] * 8, axis=0))
        train[e] = jnp.where(lane < 64, block[0:8], block[8:16]) * factor
        lefts.append(part[32:48])
        rights.append(part[48:64])
    left = jnp.concatenate(lefts, axis=0)
    right = jnp.concatenate(rights, axis=0)
    left = left + pltpu.roll(left, 64, 1)
    right = right + pltpu.roll(right, 64, 1)
    left = jnp.where(lanes_of((64, 128)) < 64, left, 0.0)
    block = exact_nt(left, jnp.concatenate([right, right], axis=0))
    same = rows_of((64, 128)) // 16 == (lanes_of((64, 128)) % 64) // 16
    block = jnp.where(same, block, 0.0)
    block = (block[0:16] + block[16:32]) + (block[32:48] + block[48:64])
    block = jnp.where(lane < 64, block[0:8], block[8:16]).astype(BF16)
    msg[...] = jnp.broadcast_to(block[None], msg.shape)


def sketch(recv, factor):
    vmem = pl.BlockSpec(memory_space=pltpu.VMEM)
    return pl.pallas_call(
        functools.partial(sketch_kernel, factor),
        out_shape=(
            jax.ShapeDtypeStruct((PLANE, 8, 128), BF16),
            jax.ShapeDtypeStruct((OWN, 8, 128), F32),
        ),
        in_specs=[vmem],
        out_specs=(vmem, vmem),
        compiler_params=pltpu.CompilerParams(vmem_limit_bytes=4 << 20),
        name="sketch",
    )(recv)


def score_kernel(gathered, train, out, wide):
    wide[...] = gathered[...].astype(F32).reshape(PLANE * 8, 128)
    totals = [None] * OWN
    for r in range(8):
        rows = wide[pl.ds(r, PLANE, stride=8), :]
        for e in range(OWN):
            more = rows * train[e, r : r + 1, :]
            totals[e] = more if r == 0 else totals[e] + more
    total = jnp.concatenate(totals, axis=0)
    row, lane = rows_of((128, 64)), lanes_of((128, 64))
    pick = (row // 16) % OWN == (lane // 16) % XL * C + lane % C
    spread = jnp.dot(
        total, pick.astype(F32), precision=lax.Precision.HIGHEST, preferred_element_type=F32
    )
    row, lane = rows_of((OWN * PLANE, 64)), lanes_of((OWN * PLANE, 64))
    spread = jnp.where(row % 16 == lane // 32 * Z + (lane // C) % Z, spread, 0.0)
    out[...] = jnp.sum(spread.reshape(LINE, 16, 64), axis=1, keepdims=True)


def score(gathered, train):
    vmem = pl.BlockSpec(memory_space=pltpu.VMEM)
    return pl.pallas_call(
        score_kernel,
        out_shape=jax.ShapeDtypeStruct((LINE, 1, 64), F32),
        in_specs=[vmem, vmem],
        out_specs=vmem,
        scratch_shapes=[pltpu.VMEM((PLANE * 8, 128), F32)],
        compiler_params=pltpu.CompilerParams(vmem_limit_bytes=4 << 20),
        name="score",
    )(gathered, train)


def exchange(x, axes):
    return lax.all_to_all(x, axes, split_axis=0, concat_axis=0, tiled=True)


def shards(
    train_hidden, train_grad, test_hidden, test_grad, proj_in, proj_out, precond_in, precond_out
):
    rank = proj_in.shape[0]
    factor = 1.0 / (rank * math.sqrt(train_hidden.shape[1] * test_hidden.shape[1]))
    send = project(
        train_hidden, train_grad, test_hidden, test_grad, proj_in, proj_out, precond_in, precond_out
    )
    recv = exchange(send, ("xl", "c", "t"))
    msg, train = sketch(recv, factor)
    gathered = exchange(msg, ("y", "z"))
    partial = score(gathered, train)
    total = exchange(partial, ("xl", "c", "t"))
    return jnp.sum(total, axis=0)


def solution(mesh):
    fine = Mesh(mesh.devices.reshape(Y, XL, Z, C, T), ("y", "xl", "z", "c", "t"))
    dp = ("y", "xl", "z", "c")
    placed = (
        P(dp, None, "t"),
        P(dp, None, "t"),
        P(dp, None, "t"),
        P(dp, None, "t"),
        P(None, "t"),
        P(None, "t"),
        P(),
        P(),
    )
    return jax.shard_map(
        shards, mesh=fine, in_specs=placed, out_specs=P(dp, "t"), check_vma=False
    )
```

```python
import functools
import math

import jax
import jax.numpy as jnp
from jax import lax
from jax.experimental import pallas as pl
from jax.experimental.pallas import tpu as pltpu
from jax.sharding import Mesh, PartitionSpec as P

Y, XL, Z, C, T = 8, 2, 8, 2, 4
OWN = XL * C
LINE = OWN * T
PLANE = Y * Z
LATE_Y, LATE_Z, LATE_T = 4, 7, 2
AXES = ("y", "xl", "z", "c", "t")
F32, BF16 = jnp.float32, jnp.bfloat16
CHUNKS = 4


def nt(a, b, precision=None):
    return lax.dot_general(
        a, b, (((1,), (1,)), ((), ())), precision=precision, preferred_element_type=F32
    )


exact_nt = functools.partial(nt, precision=lax.Precision.HIGHEST)


def lanes_of(shape):
    return lax.broadcasted_iota(jnp.int32, shape, len(shape) - 1)


def rows_of(shape):
    return lax.broadcasted_iota(jnp.int32, shape, 0)


def hi_lo(x):
    hi = x.astype(BF16)
    lo = (x - hi.astype(F32)).astype(BF16)
    return jnp.concatenate([hi, lo], axis=1)


def project_kernel(
    th, tg, qh, qg, pin, pout, cin, cout, send, th_v, tg_v, qh_v, qg_v, pin_v, pout_v, cin_v, cout_v, sems
):
    count = 0
    groups = []

    def fetch(pairs):
        nonlocal count
        started = []
        for src, dst in pairs:
            copy = pltpu.make_async_copy(src, dst, sems.at[count])
            copy.start()
            started.append(copy)
            count += 1
        groups.append(started)

    fetch([(pout, pout_v), (tg.at[0], tg_v), (qg.at[0], qg_v)])
    step = th_v.shape[1] // CHUNKS
    for k in range(CHUNKS):
        cut = pl.ds(k * step, step)
        fetch(
            [
                (pin.at[:, cut], pin_v.at[:, cut]),
                (th.at[0, :, cut], th_v.at[:, cut]),
                (qh.at[0, :, cut], qh_v.at[:, cut]),
            ]
        )
        if k == 0:
            fetch([(cin, cin_v), (cout, cout_v)])

    def wait(group):
        for copy in group:
            copy.wait()

    wait(groups[0])
    right_train = nt(pout_v[...], tg_v[...])
    right_test = nt(pout_v[...], qg_v[...])
    wait(groups[1])
    wait(groups[2])
    right_test = lax.dot_general(
        cout_v[...], right_test, (((0,), (0,)), ((), ())),
        precision=lax.Precision.HIGHEST, preferred_element_type=F32,
    )
    left_train = left_test = None
    for k in range(CHUNKS):
        if k:
            wait(groups[k + 2])
        cut = pl.ds(k * step, step)
        more_train = nt(pin_v[:, cut], th_v[:, cut])
        more_test = nt(pin_v[:, cut], qh_v[:, cut])
        left_train = more_train if k == 0 else left_train + more_train
        left_test = more_test if k == 0 else left_test + more_test
    left_test = jnp.dot(
        cin_v[...], left_test, precision=lax.Precision.HIGHEST, preferred_element_type=F32
    )
    left_train, right_train = left_train.astype(BF16), right_train.astype(BF16)
    left_test, right_test = hi_lo(left_test), hi_lo(right_test)
    for i in range(OWN):
        for j in range(T):
            peer = i * T + j
            send[peer, 0:16] = left_train[16 * i : 16 * i + 16]
            send[peer, 16:32] = right_train[16 * j : 16 * j + 16]
            send[peer, 32:48] = left_test[16 * i : 16 * i + 16]
            send[peer, 48:64] = right_test[16 * j : 16 * j + 16]


def project(th, tg, qh, qg, pin, pout, cin, cout):
    hbm = pl.BlockSpec(memory_space=pltpu.HBM)
    vmem = lambda a: pltpu.VMEM(a.shape[-2:], a.dtype)
    args = [
        pltpu.with_memory_space_constraint(a, pltpu.HBM) for a in (th, tg, qh, qg, pin, pout, cin, cout)
    ]
    return pl.pallas_call(
        project_kernel,
        out_shape=jax.ShapeDtypeStruct((LINE, 64, 128), BF16),
        in_specs=[hbm] * 8,
        out_specs=pl.BlockSpec(memory_space=pltpu.VMEM),
        scratch_shapes=[vmem(a) for a in args] + [pltpu.SemaphoreType.DMA((3 * CHUNKS + 5,))],
        compiler_params=pltpu.CompilerParams(vmem_limit_bytes=12 << 20),
        name="project",
    )(*args)


def sketch_kernel(factor, recv, msg, train):
    lane = lanes_of((8, 128))
    lefts, rights = [], []
    for e in range(OWN):
        part = recv[T * e].astype(F32)
        for t in range(1, T):
            part = part + recv[T * e + t].astype(F32)
        left, right = part[0:16], part[16:32]
        block = exact_nt(left, jnp.concatenate([right] * 8, axis=0))
        train[e] = jnp.where(lane < 64, block[0:8], block[8:16]) * factor
        lefts.append(part[32:48])
        rights.append(part[48:64])
    left = jnp.concatenate(lefts, axis=0)
    right = jnp.concatenate(rights, axis=0)
    left = left + pltpu.roll(left, 64, 1)
    right = right + pltpu.roll(right, 64, 1)
    left = jnp.where(lanes_of((64, 128)) < 64, left, 0.0)
    block = exact_nt(left, jnp.concatenate([right, right], axis=0))
    same = rows_of((64, 128)) // 16 == (lanes_of((64, 128)) % 64) // 16
    block = jnp.where(same, block, 0.0)
    block = (block[0:16] + block[16:32]) + (block[32:48] + block[48:64])
    block = jnp.where(lane < 64, block[0:8], block[8:16]).astype(BF16)
    msg[...] = jnp.broadcast_to(block[None], msg.shape)


def sketch(recv, factor):
    vmem = pl.BlockSpec(memory_space=pltpu.VMEM)
    return pl.pallas_call(
        functools.partial(sketch_kernel, factor),
        out_shape=(
            jax.ShapeDtypeStruct((PLANE, 8, 128), BF16),
            jax.ShapeDtypeStruct((OWN, 8, 128), F32),
        ),
        in_specs=[vmem],
        out_specs=(vmem, vmem),
        compiler_params=pltpu.CompilerParams(vmem_limit_bytes=4 << 20),
        name="sketch",
    )(recv)


def score_kernel(gathered, train, out, wide):
    wide[...] = gathered[...].astype(F32).reshape(PLANE * 8, 128)
    totals = [None] * OWN
    for r in range(8):
        rows = wide[pl.ds(r, PLANE, stride=8), :]
        for e in range(OWN):
            more = rows * train[e, r : r + 1, :]
            totals[e] = more if r == 0 else totals[e] + more
    total = jnp.concatenate(totals, axis=0)
    row, lane = rows_of((128, 64)), lanes_of((128, 64))
    pick = (row // 16) % OWN == (lane // 16) % XL * C + lane % C
    spread = jnp.dot(
        total, pick.astype(F32), precision=lax.Precision.HIGHEST, preferred_element_type=F32
    )
    row, lane = rows_of((OWN * PLANE, 64)), lanes_of((OWN * PLANE, 64))
    at_z = (lane // C % Z + Z - LATE_Z) % Z
    spread = jnp.where(row % 16 == lane // 32 * Z + at_z, spread, 0.0)
    out[...] = jnp.sum(spread.reshape(LINE, 16, 64), axis=1, keepdims=True)


def score(gathered, train):
    vmem = pl.BlockSpec(memory_space=pltpu.VMEM)
    return pl.pallas_call(
        score_kernel,
        out_shape=jax.ShapeDtypeStruct((LINE, 1, 64), F32),
        in_specs=[vmem, vmem],
        out_specs=vmem,
        scratch_shapes=[pltpu.VMEM((PLANE * 8, 128), F32)],
        compiler_params=pltpu.CompilerParams(vmem_limit_bytes=4 << 20),
        name="score",
    )(gathered, train)


def place(y, xl, z, c, t):
    return (((y * XL + xl) * Z + z) * C + c) * T + t


LINES = [
    [place(y, xl, z, c, (t + LATE_T) % T) for xl in range(XL) for c in range(C) for t in range(T)]
    for y in range(Y)
    for z in range(Z)
]
PLANES = [
    [place((y + LATE_Y) % Y, xl, (z + LATE_Z) % Z, c, t) for y in range(Y) for z in range(Z)]
    for xl in range(XL)
    for c in range(C)
    for t in range(T)
]


def exchange(x, groups):
    return lax.all_to_all(
        x, AXES, split_axis=0, concat_axis=0, axis_index_groups=groups, tiled=True
    )


def shards(
    train_hidden, train_grad, test_hidden, test_grad, proj_in, proj_out, precond_in, precond_out
):
    rank = proj_in.shape[0]
    factor = 1.0 / (rank * math.sqrt(train_hidden.shape[1] * test_hidden.shape[1]))
    send = project(
        train_hidden, train_grad, test_hidden, test_grad, proj_in, proj_out, precond_in, precond_out
    )
    recv = exchange(send, LINES)
    msg, train = sketch(recv, factor)
    gathered = exchange(msg, PLANES)
    partial = score(gathered, train)
    total = exchange(partial, LINES)
    return jnp.sum(total, axis=0)


def solution(mesh):
    fine = Mesh(mesh.devices.reshape(Y, XL, Z, C, T), ("y", "xl", "z", "c", "t"))
    dp = ("y", "xl", "z", "c")
    placed = (
        P(dp, None, "t"),
        P(dp, None, "t"),
        P(dp, None, "t"),
        P(dp, None, "t"),
        P(None, "t"),
        P(None, "t"),
        P(),
        P(),
    )
    return jax.shard_map(
        shards, mesh=fine, in_specs=placed, out_specs=P(dp, "t"), check_vma=False
    )
```

```python
import functools
import math

import jax
import jax.numpy as jnp
from jax import lax
from jax.experimental import pallas as pl
from jax.experimental.pallas import tpu as pltpu
from jax.sharding import Mesh, PartitionSpec as P

Y, XL, Z, C, T = 8, 2, 8, 2, 4
OWN = XL * C
LINE = OWN * T
PLANE = Y * Z
LATE_Y, LATE_Z, LATE_T = 4, 5, 2
AXES = ("y", "xl", "z", "c", "t")
F32, BF16 = jnp.float32, jnp.bfloat16
CHUNKS = 4


def nt(a, b, precision=None):
    return lax.dot_general(
        a, b, (((1,), (1,)), ((), ())), precision=precision, preferred_element_type=F32
    )


exact_nt = functools.partial(nt, precision=lax.Precision.HIGHEST)


def lanes_of(shape):
    return lax.broadcasted_iota(jnp.int32, shape, len(shape) - 1)


def rows_of(shape):
    return lax.broadcasted_iota(jnp.int32, shape, 0)


def hi_lo(x):
    hi = x.astype(BF16)
    lo = (x - hi.astype(F32)).astype(BF16)
    return jnp.concatenate([hi, lo], axis=1)


def project_kernel(
    th, tg, qh, qg, pin, pout, cin, cout, send, th_v, tg_v, qh_v, qg_v, pin_v, pout_v, cin_v, cout_v, sems
):
    count = 0
    groups = []

    def fetch(pairs):
        nonlocal count
        started = []
        for src, dst in pairs:
            copy = pltpu.make_async_copy(src, dst, sems.at[count])
            copy.start()
            started.append(copy)
            count += 1
        groups.append(started)

    fetch([(pout, pout_v), (tg.at[0], tg_v), (qg.at[0], qg_v)])
    step = th_v.shape[1] // CHUNKS
    for k in range(CHUNKS):
        cut = pl.ds(k * step, step)
        fetch(
            [
                (pin.at[:, cut], pin_v.at[:, cut]),
                (th.at[0, :, cut], th_v.at[:, cut]),
                (qh.at[0, :, cut], qh_v.at[:, cut]),
            ]
        )
        if k == 0:
            fetch([(cin, cin_v), (cout, cout_v)])

    def wait(group):
        for copy in group:
            copy.wait()

    wait(groups[0])
    right_train = nt(pout_v[...], tg_v[...])
    right_test = nt(pout_v[...], qg_v[...])
    wait(groups[1])
    wait(groups[2])
    right_test = lax.dot_general(
        cout_v[...], right_test, (((0,), (0,)), ((), ())),
        precision=lax.Precision.HIGHEST, preferred_element_type=F32,
    )
    left_train = left_test = None
    for k in range(CHUNKS):
        if k:
            wait(groups[k + 2])
        cut = pl.ds(k * step, step)
        more_train = nt(pin_v[:, cut], th_v[:, cut])
        more_test = nt(pin_v[:, cut], qh_v[:, cut])
        left_train = more_train if k == 0 else left_train + more_train
        left_test = more_test if k == 0 else left_test + more_test
    left_test = jnp.dot(
        cin_v[...], left_test, precision=lax.Precision.HIGHEST, preferred_element_type=F32
    )
    left_train, right_train = left_train.astype(BF16), right_train.astype(BF16)
    left_test, right_test = hi_lo(left_test), hi_lo(right_test)
    for i in range(OWN):
        for j in range(T):
            peer = i * T + j
            send[peer, 0:16] = left_train[16 * i : 16 * i + 16]
            send[peer, 16:32] = right_train[16 * j : 16 * j + 16]
            send[peer, 32:48] = left_test[16 * i : 16 * i + 16]
            send[peer, 48:64] = right_test[16 * j : 16 * j + 16]


def project(th, tg, qh, qg, pin, pout, cin, cout):
    hbm = pl.BlockSpec(memory_space=pltpu.HBM)
    vmem = lambda a: pltpu.VMEM(a.shape[-2:], a.dtype)
    args = [
        pltpu.with_memory_space_constraint(a, pltpu.HBM) for a in (th, tg, qh, qg, pin, pout, cin, cout)
    ]
    return pl.pallas_call(
        project_kernel,
        out_shape=jax.ShapeDtypeStruct((LINE, 64, 128), BF16),
        in_specs=[hbm] * 8,
        out_specs=pl.BlockSpec(memory_space=pltpu.VMEM),
        scratch_shapes=[vmem(a) for a in args] + [pltpu.SemaphoreType.DMA((3 * CHUNKS + 5,))],
        compiler_params=pltpu.CompilerParams(vmem_limit_bytes=12 << 20),
        name="project",
    )(*args)


def sketch_kernel(factor, recv, msg, train):
    lane = lanes_of((8, 128))
    lefts, rights = [], []
    for e in range(OWN):
        part = recv[T * e].astype(F32)
        for t in range(1, T):
            part = part + recv[T * e + t].astype(F32)
        left, right = part[0:16], part[16:32]
        block = exact_nt(left, jnp.concatenate([right] * 8, axis=0))
        train[e] = jnp.where(lane < 64, block[0:8], block[8:16]) * factor
        lefts.append(part[32:48])
        rights.append(part[48:64])
    left = jnp.concatenate(lefts, axis=0)
    right = jnp.concatenate(rights, axis=0)
    left = left + pltpu.roll(left, 64, 1)
    right = right + pltpu.roll(right, 64, 1)
    left = jnp.where(lanes_of((64, 128)) < 64, left, 0.0)
    block = exact_nt(left, jnp.concatenate([right, right], axis=0))
    same = rows_of((64, 128)) // 16 == (lanes_of((64, 128)) % 64) // 16
    block = jnp.where(same, block, 0.0)
    block = (block[0:16] + block[16:32]) + (block[32:48] + block[48:64])
    block = jnp.where(lane < 64, block[0:8], block[8:16]).astype(BF16)
    msg[...] = jnp.broadcast_to(block[None], msg.shape)


def sketch(recv, factor):
    vmem = pl.BlockSpec(memory_space=pltpu.VMEM)
    return pl.pallas_call(
        functools.partial(sketch_kernel, factor),
        out_shape=(
            jax.ShapeDtypeStruct((PLANE, 8, 128), BF16),
            jax.ShapeDtypeStruct((OWN, 8, 128), F32),
        ),
        in_specs=[vmem],
        out_specs=(vmem, vmem),
        compiler_params=pltpu.CompilerParams(vmem_limit_bytes=4 << 20),
        name="sketch",
    )(recv)


def score_kernel(gathered, train, out, wide):
    wide[...] = gathered[...].astype(F32).reshape(PLANE * 8, 128)
    totals = [None] * OWN
    for r in range(8):
        rows = wide[pl.ds(r, PLANE, stride=8), :]
        for e in range(OWN):
            more = rows * train[e, r : r + 1, :]
            totals[e] = more if r == 0 else totals[e] + more
    total = jnp.concatenate(totals, axis=0)
    row, lane = rows_of((128, 64)), lanes_of((128, 64))
    pick = (row // 16) % OWN == (lane // 16) % XL * C + lane % C
    spread = jnp.dot(
        total, pick.astype(F32), precision=lax.Precision.HIGHEST, preferred_element_type=F32
    )
    row, lane = rows_of((OWN * PLANE, 64)), lanes_of((OWN * PLANE, 64))
    at_z = (lane // C % Z + Z - LATE_Z) % Z
    spread = jnp.where(row % 16 == lane // 32 * Z + at_z, spread, 0.0)
    out[...] = jnp.sum(spread.reshape(LINE, 16, 64), axis=1, keepdims=True)


def score(gathered, train):
    vmem = pl.BlockSpec(memory_space=pltpu.VMEM)
    return pl.pallas_call(
        score_kernel,
        out_shape=jax.ShapeDtypeStruct((LINE, 1, 64), F32),
        in_specs=[vmem, vmem],
        out_specs=vmem,
        scratch_shapes=[pltpu.VMEM((PLANE * 8, 128), F32)],
        compiler_params=pltpu.CompilerParams(vmem_limit_bytes=4 << 20),
        name="score",
    )(gathered, train)


def place(y, xl, z, c, t):
    return (((y * XL + xl) * Z + z) * C + c) * T + t


LINES = [
    [place(y, xl, z, c, (t + LATE_T) % T) for xl in range(XL) for c in range(C) for t in range(T)]
    for y in range(Y)
    for z in range(Z)
]
PLANES = [
    [place((y + LATE_Y) % Y, xl, (z + LATE_Z) % Z, c, t) for y in range(Y) for z in range(Z)]
    for xl in range(XL)
    for c in range(C)
    for t in range(T)
]


def exchange(x, groups):
    return lax.all_to_all(
        x, AXES, split_axis=0, concat_axis=0, axis_index_groups=groups, tiled=True
    )


def shards(
    train_hidden, train_grad, test_hidden, test_grad, proj_in, proj_out, precond_in, precond_out
):
    rank = proj_in.shape[0]
    factor = 1.0 / (rank * math.sqrt(train_hidden.shape[1] * test_hidden.shape[1]))
    send = project(
        train_hidden, train_grad, test_hidden, test_grad, proj_in, proj_out, precond_in, precond_out
    )
    recv = exchange(send, LINES)
    msg, train = sketch(recv, factor)
    gathered = exchange(msg, PLANES)
    partial = score(gathered, train)
    total = exchange(partial, LINES)
    return jnp.sum(total, axis=0)


def solution(mesh):
    fine = Mesh(mesh.devices.reshape(Y, XL, Z, C, T), ("y", "xl", "z", "c", "t"))
    dp = ("y", "xl", "z", "c")
    placed = (
        P(dp, None, "t"),
        P(dp, None, "t"),
        P(dp, None, "t"),
        P(dp, None, "t"),
        P(None, "t"),
        P(None, "t"),
        P(),
        P(),
    )
    return jax.shard_map(
        shards, mesh=fine, in_specs=placed, out_specs=P(dp, "t"), check_vma=False
    )
```

```python
import functools
import math

import jax
import jax.numpy as jnp
from jax import lax
from jax.experimental import pallas as pl
from jax.experimental.pallas import tpu as pltpu
from jax.sharding import Mesh, PartitionSpec as P

Y, XL, Z, C, T = 8, 2, 8, 2, 4
OWN = XL * C
LINE = OWN * T
PLANE = Y * Z
LATE_Y, LATE_Z, LATE_T = 4, 5, 2
AXES = ("y", "xl", "z", "c", "t")
F32, BF16 = jnp.float32, jnp.bfloat16
PARTS = (10, 8, 6, 4)
SPLIT = 2


def nt(a, b, precision=None):
    return lax.dot_general(
        a, b, (((1,), (1,)), ((), ())), precision=precision, preferred_element_type=F32
    )


def wide_nt(a, b):
    step = a.shape[1] // SPLIT
    total = None
    for k in range(SPLIT):
        more = nt(a[:, k * step : (k + 1) * step], b[:, k * step : (k + 1) * step])
        total = more if k == 0 else total + more
    return total


exact_nt = functools.partial(nt, precision=lax.Precision.HIGHEST)


def lanes_of(shape):
    return lax.broadcasted_iota(jnp.int32, shape, len(shape) - 1)


def rows_of(shape):
    return lax.broadcasted_iota(jnp.int32, shape, 0)


def hi_lo(x):
    hi = x.astype(BF16)
    lo = (x - hi.astype(F32)).astype(BF16)
    return jnp.concatenate([hi, lo], axis=1)


def project_kernel(
    th, tg, qh, qg, pin, pout, cin, cout, send, th_v, tg_v, qh_v, qg_v, pin_v, pout_v, cin_v, cout_v, sems
):
    count = 0
    groups = []

    def fetch(pairs):
        nonlocal count
        started = []
        for src, dst in pairs:
            copy = pltpu.make_async_copy(src, dst, sems.at[count])
            copy.start()
            started.append(copy)
            count += 1
        groups.append(started)

    fetch([(pout, pout_v), (tg.at[0], tg_v), (qg.at[0], qg_v)])
    cuts, low = [], 0
    for part in PARTS:
        cuts.append(pl.ds(low, th_v.shape[1] * part // sum(PARTS)))
        low += cuts[-1].size
    for k, cut in enumerate(cuts):
        fetch(
            [
                (pin.at[:, cut], pin_v.at[:, cut]),
                (th.at[0, :, cut], th_v.at[:, cut]),
                (qh.at[0, :, cut], qh_v.at[:, cut]),
            ]
        )
        if k == 0:
            fetch([(cin, cin_v), (cout, cout_v)])

    def wait(group):
        for copy in group:
            copy.wait()

    wait(groups[0])
    right_train = wide_nt(pout_v[...], tg_v[...])
    right_test = wide_nt(pout_v[...], qg_v[...])
    wait(groups[1])
    wait(groups[2])
    right_test = lax.dot_general(
        cout_v[...], right_test, (((0,), (0,)), ((), ())),
        precision=lax.Precision.HIGHEST, preferred_element_type=F32,
    )
    left_train = left_test = None
    for k, cut in enumerate(cuts):
        if k:
            wait(groups[k + 2])
        more_train = wide_nt(pin_v[:, cut], th_v[:, cut])
        more_test = wide_nt(pin_v[:, cut], qh_v[:, cut])
        left_train = more_train if k == 0 else left_train + more_train
        left_test = more_test if k == 0 else left_test + more_test
    left_test = jnp.dot(
        cin_v[...], left_test, precision=lax.Precision.HIGHEST, preferred_element_type=F32
    )
    left_train, right_train = left_train.astype(BF16), right_train.astype(BF16)
    left_test, right_test = hi_lo(left_test), hi_lo(right_test)
    for i in range(OWN):
        for j in range(T):
            peer = i * T + j
            send[peer, 0:16] = left_train[16 * i : 16 * i + 16]
            send[peer, 16:32] = right_train[16 * j : 16 * j + 16]
            send[peer, 32:48] = left_test[16 * i : 16 * i + 16]
            send[peer, 48:64] = right_test[16 * j : 16 * j + 16]


def project(th, tg, qh, qg, pin, pout, cin, cout):
    hbm = pl.BlockSpec(memory_space=pltpu.HBM)
    vmem = lambda a: pltpu.VMEM(a.shape[-2:], a.dtype)
    args = [
        pltpu.with_memory_space_constraint(a, pltpu.HBM) for a in (th, tg, qh, qg, pin, pout, cin, cout)
    ]
    return pl.pallas_call(
        project_kernel,
        out_shape=jax.ShapeDtypeStruct((LINE, 64, 128), BF16),
        in_specs=[hbm] * 8,
        out_specs=pl.BlockSpec(memory_space=pltpu.VMEM),
        scratch_shapes=[vmem(a) for a in args] + [pltpu.SemaphoreType.DMA((3 * len(PARTS) + 5,))],
        compiler_params=pltpu.CompilerParams(vmem_limit_bytes=12 << 20),
        name="project",
    )(*args)


def sketch_kernel(factor, recv, msg, train):
    lane = lanes_of((8, 128))
    lefts, rights = [], []
    for e in range(OWN):
        part = recv[T * e].astype(F32)
        for t in range(1, T):
            part = part + recv[T * e + t].astype(F32)
        left, right = part[0:16], part[16:32]
        block = exact_nt(left, jnp.concatenate([right] * 8, axis=0))
        train[e] = jnp.where(lane < 64, block[0:8], block[8:16]) * factor
        lefts.append(part[32:48])
        rights.append(part[48:64])
    left = jnp.concatenate(lefts, axis=0)
    right = jnp.concatenate(rights, axis=0)
    left = left + pltpu.roll(left, 64, 1)
    right = right + pltpu.roll(right, 64, 1)
    left = jnp.where(lanes_of((64, 128)) < 64, left, 0.0)
    block = exact_nt(left, jnp.concatenate([right, right], axis=0))
    same = rows_of((64, 128)) // 16 == (lanes_of((64, 128)) % 64) // 16
    block = jnp.where(same, block, 0.0)
    block = (block[0:16] + block[16:32]) + (block[32:48] + block[48:64])
    block = jnp.where(lane < 64, block[0:8], block[8:16]).astype(BF16)
    msg[...] = jnp.broadcast_to(block[None], msg.shape)


def sketch(recv, factor):
    vmem = pl.BlockSpec(memory_space=pltpu.VMEM)
    return pl.pallas_call(
        functools.partial(sketch_kernel, factor),
        out_shape=(
            jax.ShapeDtypeStruct((PLANE, 8, 128), BF16),
            jax.ShapeDtypeStruct((OWN, 8, 128), F32),
        ),
        in_specs=[vmem],
        out_specs=(vmem, vmem),
        compiler_params=pltpu.CompilerParams(vmem_limit_bytes=4 << 20),
        name="sketch",
    )(recv)


def score_kernel(gathered, train, out, wide):
    wide[...] = gathered[...].astype(F32).reshape(PLANE * 8, 128)
    totals = [None] * OWN
    for r in range(8):
        rows = wide[pl.ds(r, PLANE, stride=8), :]
        for e in range(OWN):
            more = rows * train[e, r : r + 1, :]
            totals[e] = more if r == 0 else totals[e] + more
    total = jnp.concatenate(totals, axis=0)
    row, lane = rows_of((128, 64)), lanes_of((128, 64))
    pick = (row // 16) % OWN == (lane // 16) % XL * C + lane % C
    spread = jnp.dot(
        total, pick.astype(F32), precision=lax.Precision.HIGHEST, preferred_element_type=F32
    )
    row, lane = rows_of((OWN * PLANE, 64)), lanes_of((OWN * PLANE, 64))
    at_z = (lane // C % Z + Z - LATE_Z) % Z
    spread = jnp.where(row % 16 == lane // 32 * Z + at_z, spread, 0.0)
    out[...] = jnp.sum(spread.reshape(LINE, 16, 64), axis=1, keepdims=True)


def score(gathered, train):
    vmem = pl.BlockSpec(memory_space=pltpu.VMEM)
    return pl.pallas_call(
        score_kernel,
        out_shape=jax.ShapeDtypeStruct((LINE, 1, 64), F32),
        in_specs=[vmem, vmem],
        out_specs=vmem,
        scratch_shapes=[pltpu.VMEM((PLANE * 8, 128), F32)],
        compiler_params=pltpu.CompilerParams(vmem_limit_bytes=4 << 20),
        name="score",
    )(gathered, train)


def total_kernel(parts, out):
    out[...] = jnp.sum(parts[...], axis=0)


def total(parts):
    vmem = pl.BlockSpec(memory_space=pltpu.VMEM)
    return pl.pallas_call(
        total_kernel,
        out_shape=jax.ShapeDtypeStruct(parts.shape[1:], F32),
        in_specs=[vmem],
        out_specs=vmem,
        compiler_params=pltpu.CompilerParams(vmem_limit_bytes=1 << 20),
        name="total",
    )(parts)


def place(y, xl, z, c, t):
    return (((y * XL + xl) * Z + z) * C + c) * T + t


LINES = [
    [place(y, xl, z, c, (t + LATE_T) % T) for xl in range(XL) for c in range(C) for t in range(T)]
    for y in range(Y)
    for z in range(Z)
]
PLANES = [
    [place((y + LATE_Y) % Y, xl, (z + LATE_Z) % Z, c, t) for y in range(Y) for z in range(Z)]
    for xl in range(XL)
    for c in range(C)
    for t in range(T)
]


def exchange(x, groups):
    return lax.all_to_all(
        x, AXES, split_axis=0, concat_axis=0, axis_index_groups=groups, tiled=True
    )


def shards(
    train_hidden, train_grad, test_hidden, test_grad, proj_in, proj_out, precond_in, precond_out
):
    rank = proj_in.shape[0]
    factor = 1.0 / (rank * math.sqrt(train_hidden.shape[1] * test_hidden.shape[1]))
    send = project(
        train_hidden, train_grad, test_hidden, test_grad, proj_in, proj_out, precond_in, precond_out
    )
    recv = exchange(send, LINES)
    msg, train = sketch(recv, factor)
    gathered = exchange(msg, PLANES)
    partial = score(gathered, train)
    return total(exchange(partial, LINES))


def solution(mesh):
    fine = Mesh(mesh.devices.reshape(Y, XL, Z, C, T), ("y", "xl", "z", "c", "t"))
    dp = ("y", "xl", "z", "c")
    placed = (
        P(dp, None, "t"),
        P(dp, None, "t"),
        P(dp, None, "t"),
        P(dp, None, "t"),
        P(None, "t"),
        P(None, "t"),
        P(),
        P(),
    )
    return jax.shard_map(
        shards, mesh=fine, in_specs=placed, out_specs=P(dp, "t"), check_vma=False
    )
```

```python
import functools
import math

import jax
import jax.numpy as jnp
from jax import lax
from jax.experimental import pallas as pl
from jax.experimental.pallas import tpu as pltpu
from jax.sharding import Mesh, PartitionSpec as P

Y, XL, Z, C, T = 8, 2, 8, 2, 4
OWN = XL * C
LINE = OWN * T
PLANE = Y * Z
LATE_Y, LATE_Z, LATE_T = 4, 5, 2
AXES = ("y", "xl", "z", "c", "t")
F32, BF16 = jnp.float32, jnp.bfloat16
PARTS = (10, 8, 6, 4)
SPLIT = 2


def nt(a, b, precision=None):
    return lax.dot_general(
        a, b, (((1,), (1,)), ((), ())), precision=precision, preferred_element_type=F32
    )


def wide_nt(a, b):
    step = a.shape[1] // SPLIT
    total = None
    for k in range(SPLIT):
        more = nt(a[:, k * step : (k + 1) * step], b[:, k * step : (k + 1) * step])
        total = more if k == 0 else total + more
    return total


exact_nt = functools.partial(nt, precision=lax.Precision.HIGH)


def lanes_of(shape):
    return lax.broadcasted_iota(jnp.int32, shape, len(shape) - 1)


def rows_of(shape):
    return lax.broadcasted_iota(jnp.int32, shape, 0)


def hi_lo(x):
    hi = x.astype(BF16)
    lo = (x - hi.astype(F32)).astype(BF16)
    return jnp.concatenate([hi, lo], axis=1)


def project_kernel(
    th, tg, qh, qg, pin, pout, cin, cout, send, th_v, tg_v, qh_v, qg_v, pin_v, pout_v, cin_v, cout_v, sems
):
    count = 0
    groups = []

    def fetch(pairs):
        nonlocal count
        started = []
        for src, dst in pairs:
            copy = pltpu.make_async_copy(src, dst, sems.at[count])
            copy.start()
            started.append(copy)
            count += 1
        groups.append(started)

    fetch([(pout, pout_v), (tg.at[0], tg_v), (qg.at[0], qg_v)])
    cuts, low = [], 0
    for part in PARTS:
        cuts.append(pl.ds(low, th_v.shape[1] * part // sum(PARTS)))
        low += cuts[-1].size
    for k, cut in enumerate(cuts):
        fetch(
            [
                (pin.at[:, cut], pin_v.at[:, cut]),
                (th.at[0, :, cut], th_v.at[:, cut]),
                (qh.at[0, :, cut], qh_v.at[:, cut]),
            ]
        )
        if k == 0:
            fetch([(cin, cin_v), (cout, cout_v)])

    def wait(group):
        for copy in group:
            copy.wait()

    wait(groups[0])
    right_train = wide_nt(pout_v[...], tg_v[...])
    right_test = wide_nt(pout_v[...], qg_v[...])
    wait(groups[1])
    wait(groups[2])
    right_test = lax.dot_general(
        cout_v[...], right_test, (((0,), (0,)), ((), ())),
        precision=lax.Precision.HIGH, preferred_element_type=F32,
    )
    left_train = left_test = None
    for k, cut in enumerate(cuts):
        if k:
            wait(groups[k + 2])
        more_train = wide_nt(pin_v[:, cut], th_v[:, cut])
        more_test = wide_nt(pin_v[:, cut], qh_v[:, cut])
        left_train = more_train if k == 0 else left_train + more_train
        left_test = more_test if k == 0 else left_test + more_test
    left_test = jnp.dot(
        cin_v[...], left_test, precision=lax.Precision.HIGH, preferred_element_type=F32
    )
    left_train, right_train = left_train.astype(BF16), right_train.astype(BF16)
    left_test, right_test = hi_lo(left_test), hi_lo(right_test)
    for i in range(OWN):
        for j in range(T):
            peer = i * T + j
            send[peer, 0:16] = left_train[16 * i : 16 * i + 16]
            send[peer, 16:32] = right_train[16 * j : 16 * j + 16]
            send[peer, 32:48] = left_test[16 * i : 16 * i + 16]
            send[peer, 48:64] = right_test[16 * j : 16 * j + 16]


def project(th, tg, qh, qg, pin, pout, cin, cout):
    hbm = pl.BlockSpec(memory_space=pltpu.HBM)
    vmem = lambda a: pltpu.VMEM(a.shape[-2:], a.dtype)
    args = [
        pltpu.with_memory_space_constraint(a, pltpu.HBM) for a in (th, tg, qh, qg, pin, pout, cin, cout)
    ]
    return pl.pallas_call(
        project_kernel,
        out_shape=jax.ShapeDtypeStruct((LINE, 64, 128), BF16),
        in_specs=[hbm] * 8,
        out_specs=pl.BlockSpec(memory_space=pltpu.VMEM),
        scratch_shapes=[vmem(a) for a in args] + [pltpu.SemaphoreType.DMA((3 * len(PARTS) + 5,))],
        compiler_params=pltpu.CompilerParams(vmem_limit_bytes=12 << 20),
        name="project",
    )(*args)


def sketch_kernel(factor, recv, msg, train):
    lane = lanes_of((8, 128))
    lefts, rights = [], []
    for e in range(OWN):
        part = recv[T * e].astype(F32)
        for t in range(1, T):
            part = part + recv[T * e + t].astype(F32)
        left, right = part[0:16], part[16:32]
        block = exact_nt(left, jnp.concatenate([right] * 8, axis=0))
        train[e] = jnp.where(lane < 64, block[0:8], block[8:16]) * factor
        lefts.append(part[32:48])
        rights.append(part[48:64])
    left = jnp.concatenate(lefts, axis=0)
    right = jnp.concatenate(rights, axis=0)
    left = left + pltpu.roll(left, 64, 1)
    right = right + pltpu.roll(right, 64, 1)
    left = jnp.where(lanes_of((64, 128)) < 64, left, 0.0)
    block = exact_nt(left, jnp.concatenate([right, right], axis=0))
    same = rows_of((64, 128)) // 16 == (lanes_of((64, 128)) % 64) // 16
    block = jnp.where(same, block, 0.0)
    block = (block[0:16] + block[16:32]) + (block[32:48] + block[48:64])
    block = jnp.where(lane < 64, block[0:8], block[8:16]).astype(BF16)
    msg[...] = jnp.broadcast_to(block[None], msg.shape)


def sketch(recv, factor):
    vmem = pl.BlockSpec(memory_space=pltpu.VMEM)
    return pl.pallas_call(
        functools.partial(sketch_kernel, factor),
        out_shape=(
            jax.ShapeDtypeStruct((PLANE, 8, 128), BF16),
            jax.ShapeDtypeStruct((OWN, 8, 128), F32),
        ),
        in_specs=[vmem],
        out_specs=(vmem, vmem),
        compiler_params=pltpu.CompilerParams(vmem_limit_bytes=4 << 20),
        name="sketch",
    )(recv)


def score_kernel(gathered, train, out, wide):
    wide[...] = gathered[...].astype(F32).reshape(PLANE * 8, 128)
    totals = [None] * OWN
    for r in range(8):
        rows = wide[pl.ds(r, PLANE, stride=8), :]
        for e in range(OWN):
            more = rows * train[e, r : r + 1, :]
            totals[e] = more if r == 0 else totals[e] + more
    total = jnp.concatenate(totals, axis=0)
    row, lane = rows_of((128, 64)), lanes_of((128, 64))
    pick = (row // 16) % OWN == (lane // 16) % XL * C + lane % C
    spread = jnp.dot(
        total, pick.astype(F32), precision=lax.Precision.HIGH, preferred_element_type=F32
    )
    row, lane = rows_of((OWN * PLANE, 64)), lanes_of((OWN * PLANE, 64))
    at_z = (lane // C % Z + Z - LATE_Z) % Z
    spread = jnp.where(row % 16 == lane // 32 * Z + at_z, spread, 0.0)
    out[...] = jnp.sum(spread.reshape(LINE, 16, 64), axis=1, keepdims=True)


def score(gathered, train):
    vmem = pl.BlockSpec(memory_space=pltpu.VMEM)
    return pl.pallas_call(
        score_kernel,
        out_shape=jax.ShapeDtypeStruct((LINE, 1, 64), F32),
        in_specs=[vmem, vmem],
        out_specs=vmem,
        scratch_shapes=[pltpu.VMEM((PLANE * 8, 128), F32)],
        compiler_params=pltpu.CompilerParams(vmem_limit_bytes=4 << 20),
        name="score",
    )(gathered, train)


def total_kernel(parts, out):
    out[...] = jnp.sum(parts[...], axis=0)


def total(parts):
    vmem = pl.BlockSpec(memory_space=pltpu.VMEM)
    return pl.pallas_call(
        total_kernel,
        out_shape=jax.ShapeDtypeStruct(parts.shape[1:], F32),
        in_specs=[vmem],
        out_specs=vmem,
        compiler_params=pltpu.CompilerParams(vmem_limit_bytes=1 << 20),
        name="total",
    )(parts)


def place(y, xl, z, c, t):
    return (((y * XL + xl) * Z + z) * C + c) * T + t


LINES = [
    [place(y, xl, z, c, (t + LATE_T) % T) for xl in range(XL) for c in range(C) for t in range(T)]
    for y in range(Y)
    for z in range(Z)
]
PLANES = [
    [place((y + LATE_Y) % Y, xl, (z + LATE_Z) % Z, c, t) for y in range(Y) for z in range(Z)]
    for xl in range(XL)
    for c in range(C)
    for t in range(T)
]


def exchange(x, groups):
    return lax.all_to_all(
        x, AXES, split_axis=0, concat_axis=0, axis_index_groups=groups, tiled=True
    )


def shards(
    train_hidden, train_grad, test_hidden, test_grad, proj_in, proj_out, precond_in, precond_out
):
    rank = proj_in.shape[0]
    factor = 1.0 / (rank * math.sqrt(train_hidden.shape[1] * test_hidden.shape[1]))
    send = project(
        train_hidden, train_grad, test_hidden, test_grad, proj_in, proj_out, precond_in, precond_out
    )
    recv = exchange(send, LINES)
    msg, train = sketch(recv, factor)
    gathered = exchange(msg, PLANES)
    partial = score(gathered, train)
    return total(exchange(partial, LINES))


def solution(mesh):
    fine = Mesh(mesh.devices.reshape(Y, XL, Z, C, T), ("y", "xl", "z", "c", "t"))
    dp = ("y", "xl", "z", "c")
    placed = (
        P(dp, None, "t"),
        P(dp, None, "t"),
        P(dp, None, "t"),
        P(dp, None, "t"),
        P(None, "t"),
        P(None, "t"),
        P(),
        P(),
    )
    return jax.shard_map(
        shards, mesh=fine, in_specs=placed, out_specs=P(dp, "t"), check_vma=False
    )
```

```python
import functools
import math

import jax
import jax.numpy as jnp
from jax import lax
from jax.experimental import pallas as pl
from jax.experimental.pallas import tpu as pltpu
from jax.sharding import Mesh, PartitionSpec as P

Y, XL, Z, C, T = 8, 2, 8, 2, 4
OWN = XL * C
LINE = OWN * T
PLANE = Y * Z
LATE_Y, LATE_Z, LATE_T = 4, 5, 2
AXES = ("y", "xl", "z", "c", "t")
F32, BF16 = jnp.float32, jnp.bfloat16
PARTS = (10, 8, 6, 4)
SPLIT = 2


def nt(a, b, precision=None):
    return lax.dot_general(
        a, b, (((1,), (1,)), ((), ())), precision=precision, preferred_element_type=F32
    )


def wide_nt(a, b):
    step = a.shape[1] // SPLIT
    total = None
    for k in range(SPLIT):
        more = nt(a[:, k * step : (k + 1) * step], b[:, k * step : (k + 1) * step])
        total = more if k == 0 else total + more
    return total


exact_nt = functools.partial(nt, precision=lax.Precision.HIGH)


def lanes_of(shape):
    return lax.broadcasted_iota(jnp.int32, shape, len(shape) - 1)


def rows_of(shape):
    return lax.broadcasted_iota(jnp.int32, shape, 0)


def hi_lo(x):
    hi = x.astype(BF16)
    lo = (x - hi.astype(F32)).astype(BF16)
    return jnp.concatenate([hi, lo], axis=1)


def project_kernel(
    th, tg, qh, qg, pin, pout, cin, cout, send, th_v, tg_v, qh_v, qg_v, pin_v, pout_v, cin_v, cout_v, sems
):
    count = 0
    groups = []

    def fetch(pairs):
        nonlocal count
        started = []
        for src, dst in pairs:
            copy = pltpu.make_async_copy(src, dst, sems.at[count])
            copy.start()
            started.append(copy)
            count += 1
        groups.append(started)

    fetch([(pout, pout_v), (tg.at[0], tg_v), (qg.at[0], qg_v)])
    cuts, low = [], 0
    for part in PARTS:
        cuts.append(pl.ds(low, th_v.shape[1] * part // sum(PARTS)))
        low += cuts[-1].size
    for k, cut in enumerate(cuts):
        fetch(
            [
                (pin.at[:, cut], pin_v.at[:, cut]),
                (th.at[0, :, cut], th_v.at[:, cut]),
                (qh.at[0, :, cut], qh_v.at[:, cut]),
            ]
        )
        if k == 0:
            fetch([(cin, cin_v), (cout, cout_v)])

    def wait(group):
        for copy in group:
            copy.wait()

    wait(groups[0])
    right_train = wide_nt(pout_v[...], tg_v[...])
    right_test = wide_nt(pout_v[...], qg_v[...])
    wait(groups[1])
    wait(groups[2])
    right_test = lax.dot_general(
        cout_v[...], right_test, (((0,), (0,)), ((), ())),
        precision=lax.Precision.HIGH, preferred_element_type=F32,
    )
    left_train = left_test = None
    for k, cut in enumerate(cuts):
        if k:
            wait(groups[k + 2])
        more_train = wide_nt(pin_v[:, cut], th_v[:, cut])
        more_test = wide_nt(pin_v[:, cut], qh_v[:, cut])
        left_train = more_train if k == 0 else left_train + more_train
        left_test = more_test if k == 0 else left_test + more_test
    left_test = jnp.dot(
        cin_v[...], left_test, precision=lax.Precision.HIGH, preferred_element_type=F32
    )
    left_train, right_train = left_train.astype(BF16), right_train.astype(BF16)
    left_test, right_test = hi_lo(left_test), hi_lo(right_test)
    for i in range(OWN):
        for j in range(T):
            peer = i * T + j
            send[peer, 0:16] = left_train[16 * i : 16 * i + 16]
            send[peer, 16:32] = right_train[16 * j : 16 * j + 16]
            send[peer, 32:48] = left_test[16 * i : 16 * i + 16]
            send[peer, 48:64] = right_test[16 * j : 16 * j + 16]


def project(th, tg, qh, qg, pin, pout, cin, cout):
    hbm = pl.BlockSpec(memory_space=pltpu.HBM)
    vmem = lambda a: pltpu.VMEM(a.shape[-2:], a.dtype)
    args = [
        pltpu.with_memory_space_constraint(a, pltpu.HBM) for a in (th, tg, qh, qg, pin, pout, cin, cout)
    ]
    return pl.pallas_call(
        project_kernel,
        out_shape=jax.ShapeDtypeStruct((LINE, 64, 128), BF16),
        in_specs=[hbm] * 8,
        out_specs=pl.BlockSpec(memory_space=pltpu.VMEM),
        scratch_shapes=[vmem(a) for a in args] + [pltpu.SemaphoreType.DMA((3 * len(PARTS) + 5,))],
        compiler_params=pltpu.CompilerParams(vmem_limit_bytes=12 << 20),
        name="project",
    )(*args)


def sketch_kernel(factor, recv, msg, train):
    lane = lanes_of((8, 128))
    lefts, rights = [], []
    for e in range(OWN):
        part = recv[T * e].astype(F32)
        for t in range(1, T):
            part = part + recv[T * e + t].astype(F32)
        left, right = part[0:16], part[16:32]
        block = exact_nt(left, jnp.concatenate([right] * 8, axis=0))
        train[e] = jnp.where(lane < 64, block[0:8], block[8:16]) * factor
        lefts.append(part[32:48])
        rights.append(part[48:64])
    left = jnp.concatenate(lefts, axis=0)
    right = jnp.concatenate(rights, axis=0)
    left = left + pltpu.roll(left, 64, 1)
    right = right + pltpu.roll(right, 64, 1)
    left = jnp.where(lanes_of((64, 128)) < 64, left, 0.0)
    block = exact_nt(left, jnp.concatenate([right, right], axis=0))
    same = rows_of((64, 128)) // 16 == (lanes_of((64, 128)) % 64) // 16
    block = jnp.where(same, block, 0.0)
    block = (block[0:16] + block[16:32]) + (block[32:48] + block[48:64])
    block = jnp.where(lane < 64, block[0:8], block[8:16]).astype(BF16)
    msg[...] = jnp.broadcast_to(block[None], msg.shape)


def sketch(recv, factor):
    vmem = pl.BlockSpec(memory_space=pltpu.VMEM)
    return pl.pallas_call(
        functools.partial(sketch_kernel, factor),
        out_shape=(
            jax.ShapeDtypeStruct((PLANE, 8, 128), BF16),
            jax.ShapeDtypeStruct((OWN, 8, 128), F32),
        ),
        in_specs=[vmem],
        out_specs=(vmem, vmem),
        compiler_params=pltpu.CompilerParams(vmem_limit_bytes=4 << 20),
        name="sketch",
    )(recv)


def score_kernel(gathered, train, out, wide):
    wide[...] = gathered[...].astype(F32).reshape(PLANE * 8, 128)
    totals = [None] * OWN
    for r in range(8):
        rows = wide[pl.ds(r, PLANE, stride=8), :]
        for e in range(OWN):
            more = rows * train[e, r : r + 1, :]
            totals[e] = more if r == 0 else totals[e] + more
    total = jnp.concatenate([totals[e ^ 1] for e in range(OWN)], axis=0)
    row, lane = rows_of((128, 64)), lanes_of((128, 64))
    pick = (row // 16) % OWN == (lane // 16) % XL * C + lane % C
    spread = jnp.dot(
        total, pick.astype(F32), precision=lax.Precision.HIGH, preferred_element_type=F32
    )
    row, lane = rows_of((OWN * PLANE, 64)), lanes_of((OWN * PLANE, 64))
    at_z = (lane // C % Z + Z - LATE_Z) % Z
    spread = jnp.where(row % 16 == lane // 32 * Z + at_z, spread, 0.0)
    out[...] = jnp.sum(spread.reshape(LINE, 16, 64), axis=1, keepdims=True)


def score(gathered, train):
    vmem = pl.BlockSpec(memory_space=pltpu.VMEM)
    return pl.pallas_call(
        score_kernel,
        out_shape=jax.ShapeDtypeStruct((LINE, 1, 64), F32),
        in_specs=[vmem, vmem],
        out_specs=vmem,
        scratch_shapes=[pltpu.VMEM((PLANE * 8, 128), F32)],
        compiler_params=pltpu.CompilerParams(vmem_limit_bytes=4 << 20),
        name="score",
    )(gathered, train)


def total_kernel(parts, out):
    out[...] = jnp.sum(parts[...], axis=0)


def total(parts):
    vmem = pl.BlockSpec(memory_space=pltpu.VMEM)
    return pl.pallas_call(
        total_kernel,
        out_shape=jax.ShapeDtypeStruct(parts.shape[1:], F32),
        in_specs=[vmem],
        out_specs=vmem,
        compiler_params=pltpu.CompilerParams(vmem_limit_bytes=1 << 20),
        name="total",
    )(parts)


def place(y, xl, z, c, t):
    return (((y * XL + xl) * Z + z) * C + c) * T + t


LINES = [
    [place(y, xl, z, c, (t + LATE_T) % T) for xl in range(XL) for c in range(C) for t in range(T)]
    for y in range(Y)
    for z in range(Z)
]
LAST_LINES = [
    [place(y, xl, z, C - 1 - c, (t + LATE_T) % T) for xl in range(XL) for c in range(C) for t in range(T)]
    for y in range(Y)
    for z in range(Z)
]
PLANES = [
    [place((y + LATE_Y) % Y, xl, (z + LATE_Z) % Z, c, t) for y in range(Y) for z in range(Z)]
    for xl in range(XL)
    for c in range(C)
    for t in range(T)
]


def exchange(x, groups):
    return lax.all_to_all(
        x, AXES, split_axis=0, concat_axis=0, axis_index_groups=groups, tiled=True
    )


def shards(
    train_hidden, train_grad, test_hidden, test_grad, proj_in, proj_out, precond_in, precond_out
):
    rank = proj_in.shape[0]
    factor = 1.0 / (rank * math.sqrt(train_hidden.shape[1] * test_hidden.shape[1]))
    send = project(
        train_hidden, train_grad, test_hidden, test_grad, proj_in, proj_out, precond_in, precond_out
    )
    recv = exchange(send, LINES)
    msg, train = sketch(recv, factor)
    gathered = exchange(msg, PLANES)
    partial = score(gathered, train)
    return total(exchange(partial, LAST_LINES))


def solution(mesh):
    fine = Mesh(mesh.devices.reshape(Y, XL, Z, C, T), ("y", "xl", "z", "c", "t"))
    dp = ("y", "xl", "z", "c")
    placed = (
        P(dp, None, "t"),
        P(dp, None, "t"),
        P(dp, None, "t"),
        P(dp, None, "t"),
        P(None, "t"),
        P(None, "t"),
        P(),
        P(),
    )
    return jax.shard_map(
        shards, mesh=fine, in_specs=placed, out_specs=P(dp, "t"), check_vma=False
    )
```
